256 devices in a mesh: row: 16 (over z_hi, y, core), col: 16 (over x, z_lo).
Axes of the slice: x: 4, y: 4, z: 8 (z_hi: 2, z_lo: 4; z = z_hi * 4 + z_lo), core: 2. Of those that a mesh axis runs over, the one named last changes fastest.
Arguments:
- coords: float32 [64, 32768], P(None, ('row', 'col')), may hold values from -6 to 6
- dissimilarity: float32 [32768, 16384], P('row', 'col'), as said below
Outputs:
- updated: float32 [64, 32768], P(None, ('row', 'col'))
The draws below stay inside these ranges and needn't reach their ends.
Inputs may be any that keep to these rules, and one draw needn't show every extreme that they name: `dissimilarity`: each unordered pair of distinct samples appears in exactly one entry, placed as the steps state; the entries that name no pair are positive too.
All inputs are finite; a program needn't handle non-finite values.
Results may differ from the reference program's by a relative error of at most 0.0003.
Values sent between devices are 32-bit elements; how exact they have to be, the bound alone decides.
No kernel may reach another device: no remote copies, remote signals or barrier semaphores. Data moves between devices by JAX's collectives and lax.ppermute only.
A program may use at most 128 MiB of HBM per device.

```python
import math
import jax
import jax.numpy as jnp
from jax import lax

DIMS = 64
COLS = 2048
ITERS = 2
SAMPLES = 32768


def latent_spacing(leading, trailing):
    inner_prod = jnp.dot(leading.T, trailing, precision=lax.Precision.HIGHEST)
    leading_norms = jnp.sum(leading * leading, axis=0)
    trailing_norms = jnp.sum(trailing * trailing, axis=0)
    return jnp.sqrt(jnp.maximum(leading_norms[:, None] + trailing_norms[None, :] - 2.0 * inner_prod, 0.0) + 1.0)


def draw_dissimilarity(key, part):
    latent_key = jax.random.fold_in(key, 21)
    jitter_key = jax.random.fold_in(key, 22)
    block_count = SAMPLES // COLS
    half_width = COLS // 2
    latent = jax.random.normal(latent_key, (DIMS, SAMPLES), jnp.float32)
    weights = jnp.ones((SAMPLES,), jnp.float32)
    grouped = latent.reshape(DIMS, block_count, COLS)
    grouped_weights = weights.reshape(block_count, COLS)
    row_iota = lax.broadcasted_iota(jnp.int32, (COLS, half_width), 0)
    col_iota = lax.broadcasted_iota(jnp.int32, (COLS, half_width), 1)

    def one_row(row_index):
        rows_coords = lax.dynamic_index_in_dim(grouped, row_index, 1, keepdims=False)
        rows_weights = lax.dynamic_index_in_dim(grouped_weights, row_index, 0, keepdims=False)

        def one_tile(col_index):
            cols_coords = lax.dynamic_index_in_dim(grouped, col_index, 1, keepdims=False)
            cols_weights = lax.dynamic_index_in_dim(grouped_weights, col_index, 0, keepdims=False)
            row_first = row_index <= col_index
            offset = jnp.where(row_first, 0, half_width).astype(jnp.int32)
            leading = jnp.where(row_first, rows_coords, cols_coords)
            trailing = lax.dynamic_slice_in_dim(jnp.where(row_first, cols_coords, rows_coords), offset, half_width, 1)
            leading_weights = jnp.where(row_first, rows_weights, cols_weights)
            trailing_weights = lax.dynamic_slice_in_dim(jnp.where(row_first, cols_weights, rows_weights), offset, half_width, 0)
            scaled = latent_spacing(leading, trailing) * jnp.sqrt(leading_weights[:, None] * trailing_weights[None, :])
            late_coords = rows_coords[:, half_width:]
            late_weights = rows_weights[half_width:]
            late = latent_spacing(late_coords, late_coords) * jnp.sqrt(late_weights[:, None] * late_weights[None, :])
            late_full = jnp.concatenate([late, jnp.zeros_like(late)], axis=0)
            swap_mask = (row_index == col_index) & (row_iota < half_width) & (col_iota < row_iota)
            base = jnp.where(swap_mask, late_full, scaled)
            jitter = jax.random.uniform(jax.random.fold_in(jitter_key, row_index * block_count + col_index), (COLS, half_width), jnp.float32)
            return base * jnp.exp(math.log(2.0) * (2.0 * jitter - 1.0))
        return lax.map(one_tile, jnp.arange(block_count, dtype=jnp.int32))
    stacked = lax.map(one_row, jnp.arange(block_count, dtype=jnp.int32))
    return stacked.transpose(0, 2, 1, 3).reshape(SAMPLES, SAMPLES // 2).astype(jnp.float32)


def levels(own_key, dims, cuts, smallest, high):
    def one(axis_at, parts):
        heights = jax.random.uniform(jax.random.fold_in(jax.random.fold_in(own_key, 6), axis_at), (parts,), jnp.float32, smallest / len(cuts), high / len(cuts))
        return jnp.repeat(jnp.exp(heights), dims[axis_at] // parts).reshape((-1,) + (1,) * (len(dims) - axis_at - 1))

    factor_of = one(*cuts[0])
    for cut in cuts[1:]:
        factor_of = factor_of * one(*cut)
    return factor_of


def scatter_about(stream_key, dims, width, most, pieces=(), held_as=jnp.bfloat16):
    gain = levels(stream_key, dims, pieces, -0.22, 0.18) if pieces else 1.0
    drawn = jax.random.normal(stream_key, dims, jnp.float32) * width * gain
    return jnp.minimum(jnp.maximum(drawn, -most), most).astype(held_as)


def setup_inputs(seed: int = 0) -> dict:
    key_of = jax.random.split(jax.random.key(seed), 3)
    coords = scatter_about(key_of[0], (DIMS, SAMPLES), 1.0, 6.0, ((1, 256),), jnp.float32)
    dissimilarity = draw_dissimilarity(jax.random.fold_in(key_of[2], 71), 0)
    return dict(coords=coords, dissimilarity=dissimilarity)


def compute_ratios(values, leading, trailing):
    inner_prod = lax.dot_general(leading, trailing, (((0,), (0,)), ((), ())), precision=lax.Precision.HIGHEST, preferred_element_type=jnp.float32)
    leading_norms = lax.optimization_barrier(jnp.sum(leading * leading, axis=0))
    trailing_norms = lax.optimization_barrier(jnp.sum(trailing * trailing, axis=0))
    spacing = jnp.sqrt(leading_norms[:, None] + trailing_norms[None, :] - 2.0 * inner_prod + 1.0)
    return values / spacing

def pair_terms(leading, trailing, ratios):
    pulled = lax.dot_general(trailing, ratios, (((1,), (1,)), ((), ())), precision=lax.Precision.HIGHEST, preferred_element_type=jnp.float32)
    pushed = lax.dot_general(leading, ratios, (((1,), (0,)), ((), ())), precision=lax.Precision.HIGHEST, preferred_element_type=jnp.float32)
    leading_terms = leading * lax.optimization_barrier(jnp.sum(ratios, axis=1))[None, :] - pulled
    trailing_terms = trailing * lax.optimization_barrier(jnp.sum(ratios, axis=0))[None, :] - pushed
    return (leading_terms, trailing_terms)

def offdiagonal_terms(values, rows_coords, cols_coords, row_first):
    half_width = values.shape[1]
    leading = jnp.where(row_first, rows_coords, cols_coords)
    partner = jnp.where(row_first, cols_coords, rows_coords)
    offset = jnp.where(row_first, 0, half_width).astype(jnp.int32)
    trailing = lax.dynamic_slice_in_dim(partner, offset, half_width, 1)
    ratios = compute_ratios(values, leading, trailing)
    leading_terms, trailing_terms = pair_terms(leading, trailing, ratios)
    placed = lax.dynamic_update_slice_in_dim(jnp.zeros_like(partner), trailing_terms, offset, 1)
    return (jnp.where(row_first, leading_terms, placed), jnp.where(row_first, placed, leading_terms))

def diagonal_terms(values, rows_coords, cols_coords, row_first):
    half_width = values.shape[1]
    first_half = rows_coords[:, :half_width]
    second_half = rows_coords[:, half_width:]
    upper_values = values[:half_width]
    lower_values = values[half_width:]
    row_iota = lax.broadcasted_iota(jnp.int32, (half_width, half_width), 0)
    col_iota = lax.broadcasted_iota(jnp.int32, (half_width, half_width), 1)
    cross = compute_ratios(lower_values, second_half, first_half)
    cross_second, cross_first = pair_terms(second_half, first_half, cross)
    early = jnp.where(col_iota > row_iota, compute_ratios(upper_values, first_half, first_half), 0.0)
    late = jnp.where(col_iota < row_iota, compute_ratios(upper_values, second_half, second_half), 0.0)
    early_rows, early_cols = pair_terms(first_half, first_half, early)
    late_rows, late_cols = pair_terms(second_half, second_half, late)
    row_share = jnp.concatenate([early_rows + early_cols + cross_first, late_rows + late_cols + cross_second], axis=1)
    return (row_share, jnp.zeros_like(row_share))

def tile_terms(values, rows_coords, cols_coords, row_index, col_index):
    return lax.cond(row_index == col_index, diagonal_terms, offdiagonal_terms, values, rows_coords, cols_coords, row_index < col_index)

def reference(coords, dissimilarity):
    sample_count = coords.shape[1]
    block_count = sample_count // COLS
    half_width = COLS // 2
    tiles = dissimilarity.reshape(block_count, COLS, block_count, half_width)
    current = coords
    for iteration in range(ITERS):
        grouped = current.reshape(DIMS, block_count, COLS)

        def one_row(partials, row_index):
            rows_coords = lax.dynamic_index_in_dim(grouped, row_index, 1, keepdims=False)
            row_tiles = lax.dynamic_index_in_dim(tiles, row_index, 0, keepdims=False)

            def one_tile(col_index):
                values = lax.dynamic_index_in_dim(row_tiles, col_index, 1, keepdims=False)
                cols_coords = lax.dynamic_index_in_dim(grouped, col_index, 1, keepdims=False)
                return tile_terms(values, rows_coords, cols_coords, row_index, col_index)
            row_shares, col_shares = lax.map(one_tile, jnp.arange(block_count, dtype=jnp.int32))
            partials = partials + jnp.transpose(col_shares, (1, 0, 2))
            own_row = lax.dynamic_index_in_dim(partials, row_index, 1, keepdims=False) + lax.optimization_barrier(jnp.sum(row_shares, axis=0))
            partials = lax.dynamic_update_index_in_dim(partials, own_row, row_index, 1)
            return (partials, None)
        initial = jnp.zeros((DIMS, block_count, COLS), jnp.float32)
        summed, _ = lax.scan(one_row, initial, jnp.arange(block_count, dtype=jnp.int32))
        current = summed.reshape(DIMS, sample_count) / sample_count
    return current
```

```python
import jax
import jax.numpy as jnp
from jax import lax
from jax.experimental import pallas as pl
from jax.experimental.pallas import tpu as pltpu
from jax.sharding import PartitionSpec as P

ITERS = 2
DIMS = 64
PIECE = 128
CHUNK = 256
HALF = 4
BLOCK = 8
STACK = 3 * DIMS + 16
SAMPLES = 32768

X_GROUPS = [[z + 4 * x for x in range(4)] for z in range(4)]
Z_GROUPS = [[4 * x + z for z in range(4)] for x in range(4)]
YC_GROUPS = [list(range(8)), list(range(8, 16))]


def nn(a, b):
    return lax.dot_general(a, b, (((1,), (0,)), ((), ())), preferred_element_type=jnp.float32)


def nt(a, b):
    return lax.dot_general(a, b, (((1,), (1,)), ((), ())), preferred_element_type=jnp.float32)


def tile_kernel(where_ref, values_ref, rows_ref, cols_ref, row_out, col_out, left, right, stack, norm_i, norm_j, acc):
    step = pl.program_id(0)
    lead_base, trail_base, diagonal = where_ref[0], where_ref[1], where_ref[2]

    def coords_of(n):
        ref, m = (rows_ref, n) if n < BLOCK else (cols_ref, n - BLOCK)
        return jnp.concatenate([ref[2 * m], ref[2 * m + 1]], axis=1)

    @pl.when(step == 0)
    def _():
        acc[...] = jnp.zeros_like(acc)
        ones = jnp.ones((16, CHUNK), jnp.bfloat16)
        for n in range(2 * BLOCK):
            x = coords_of(n)
            hi = x.astype(jnp.bfloat16)
            rest = x - hi.astype(jnp.float32)
            mid = rest.astype(jnp.bfloat16)
            lo = (rest - mid.astype(jnp.float32)).astype(jnp.bfloat16)
            stack[n] = jnp.concatenate([hi, mid, lo, ones], axis=0)
            right[n] = -2.0 * jnp.concatenate([hi, mid, mid, hi], axis=0)
            hi32, mid32 = hi.astype(jnp.float32), mid.astype(jnp.float32)
            flipped = jnp.concatenate([hi32, mid32], axis=0).T
            flipped16 = flipped.astype(jnp.bfloat16)
            left[n] = jnp.concatenate([flipped16, flipped16], axis=1)
            near = hi32 + mid32
            norm_j[n] = jnp.broadcast_to(jnp.sum(near * near, axis=0, keepdims=True) + 1.0, (8, CHUNK))
            turned = near.T
            norm_i[n] = jnp.broadcast_to(jnp.sum(turned * turned, axis=1, keepdims=True), (CHUNK, PIECE))

    def ratios_of(values, lead, trail):
        inner = nn(left[lead], right[trail])
        ni = norm_i[lead]
        squared = inner + (jnp.concatenate([ni, ni], axis=1) + norm_j[trail, 0:1, :])
        return values * lax.rsqrt(squared)

    def products(ratios, lead, trail):
        hi = ratios.astype(jnp.bfloat16)
        lo = (ratios - hi.astype(jnp.float32)).astype(jnp.bfloat16)
        acc[trail] += nn(stack[lead], hi) + nn(stack[lead], lo)
        return nt(stack[trail], hi) + nt(stack[trail], lo)

    special = jnp.logical_and(diagonal == 1, step < HALF)

    @pl.when(jnp.logical_not(special))
    def _():
        lead = lead_base + step
        pulled = None
        for j in range(HALF):
            trail = trail_base + j
            ratios = ratios_of(values_ref[:, j * CHUNK : (j + 1) * CHUNK], lead, trail)
            part = products(ratios, lead, trail)
            pulled = part if pulled is None else pulled + part
        acc[lead] += pulled

    @pl.when(special)
    def _():
        row_iota = lax.broadcasted_iota(jnp.int32, (CHUNK, CHUNK), 0)
        col_iota = lax.broadcasted_iota(jnp.int32, (CHUNK, CHUNK), 1)
        for j in range(HALF):
            values = values_ref[:, j * CHUNK : (j + 1) * CHUNK]

            @pl.when(step != j)
            def _():
                shift = jnp.where(step > j, HALF, 0)
                lead, trail = step + shift, j + shift
                ratios = ratios_of(values, lead, trail)
                pulled = products(ratios, lead, trail)
                acc[lead] += pulled

            @pl.when(step == j)
            def _():
                for shift, keep in ((0, col_iota > row_iota), (HALF, col_iota < row_iota)):
                    ratios = jnp.where(keep, ratios_of(values, j + shift, j + shift), 0.0)
                    pulled = products(ratios, j + shift, j + shift)
                    acc[j + shift] += pulled

    @pl.when(step == BLOCK - 1)
    def _():
        for n in range(2 * BLOCK):
            x = coords_of(n)
            pulled = acc[n, 0:DIMS] + acc[n, DIMS : 2 * DIMS] + acc[n, 2 * DIMS : 3 * DIMS]
            terms = x * acc[n, 3 * DIMS : 3 * DIMS + 1] - pulled
            out, m = (row_out, n) if n < BLOCK else (col_out, n - BLOCK)
            out[2 * m] = terms[:, :PIECE]
            out[2 * m + 1] = terms[:, PIECE:]


def tile_terms(where, values, rows, cols):
    pieces = jax.ShapeDtypeStruct(rows.shape, jnp.float32)
    whole = pl.BlockSpec(rows.shape, lambda i, w: (0, 0, 0))
    return pl.pallas_call(
        tile_kernel,
        out_shape=(pieces, pieces),
        grid_spec=pltpu.PrefetchScalarGridSpec(
            num_scalar_prefetch=1,
            grid=(BLOCK,),
            in_specs=[pl.BlockSpec((CHUNK, values.shape[1]), lambda i, w: (i, 0)), whole, whole],
            out_specs=(whole, whole),
            scratch_shapes=[
                pltpu.VMEM((2 * BLOCK, CHUNK, CHUNK), jnp.bfloat16),
                pltpu.VMEM((2 * BLOCK, CHUNK, CHUNK), jnp.bfloat16),
                pltpu.VMEM((2 * BLOCK, STACK, CHUNK), jnp.bfloat16),
                pltpu.VMEM((2 * BLOCK, CHUNK, PIECE), jnp.float32),
                pltpu.VMEM((2 * BLOCK, 8, CHUNK), jnp.float32),
                pltpu.VMEM((2 * BLOCK, STACK, CHUNK), jnp.float32),
            ],
        ),
        compiler_params=pltpu.CompilerParams(
            dimension_semantics=("arbitrary",), vmem_limit_bytes=40 * 1024 * 1024
        ),
        cost_estimate=pl.CostEstimate(flops=6_000_000_000, transcendentals=2_097_152, bytes_accessed=10_000_000),
    )(where, values, rows, cols)


def exchange(x, axis, groups):
    return lax.all_to_all(x, axis, split_axis=0, concat_axis=0, tiled=True, axis_index_groups=groups)


def spread(x, axis, groups):
    return exchange(jnp.broadcast_to(x, (len(groups[0]), *x.shape)), axis, groups)


def transposed(x):
    pairs = [(a * 16 + b, b * 16 + a) for a in range(16) for b in range(16)]
    return lax.ppermute(x, ("row", "col"), pairs)


def across(x):
    return lax.ppermute(x, "row", [(a, (a + 8) % 16) for a in range(16)])


def gathered(own, turned, low):
    other = across(turned)
    line = spread(own, "col", Z_GROUPS)
    rows = spread(line, "col", X_GROUPS).reshape(16, DIMS, PIECE)
    both = jnp.stack([jnp.where(low, turned, other), jnp.where(low, other, turned)])
    cols = spread(both, "row", YC_GROUPS)
    return rows, jnp.swapaxes(cols, 0, 1).reshape(16, DIMS, PIECE)


def reduced(row_part, col_part, low):
    halves = jnp.swapaxes(col_part.reshape(2, 8, DIMS, PIECE), 0, 1)
    halves = exchange(halves, "row", YC_GROUPS).sum(axis=0)
    kept = jnp.where(low, halves[0], halves[1])
    sent = jnp.where(low, halves[1], halves[0])
    came = across(sent)
    line = exchange(row_part.reshape(4, 4, DIMS, PIECE), "col", X_GROUPS).sum(axis=0)
    row_sum = exchange(line, "col", Z_GROUPS).sum(axis=0)
    return row_sum, kept + came


def local(coords, dissimilarity):
    row, col = lax.axis_index("row"), lax.axis_index("col")
    low = row < 8
    lead_base = jnp.where(row > col, BLOCK, 0)
    trail_base = jnp.where(row < col, BLOCK, jnp.where(row > col, HALF, 0))
    where = jnp.stack([lead_base, trail_base, (row == col).astype(jnp.int32)]).astype(jnp.int32)
    own, turned = coords, transposed(coords)
    scale = 1.0 / SAMPLES
    for iteration in range(ITERS):
        rows, cols = gathered(own, turned, low)
        row_part, col_part = tile_terms(where, dissimilarity, rows, cols)
        row_sum, col_sum = reduced(row_part, col_part, low)
        if iteration + 1 < ITERS:
            came = transposed(jnp.stack([row_sum, col_sum]))
            own = (row_sum + came[1]) * scale
            turned = (col_sum + came[0]) * scale
        else:
            own = (row_sum + transposed(col_sum)) * scale
    return own


def solution(mesh):
    in_specs = (P(None, ("row", "col")), P("row", "col"))
    out_specs = P(None, ("row", "col"))
    return jax.shard_map(local, mesh=mesh, in_specs=in_specs, out_specs=out_specs, check_vma=False)
```

```python
import jax
import jax.numpy as jnp
from jax import lax
from jax.experimental import pallas as pl
from jax.experimental.pallas import tpu as pltpu
from jax.sharding import PartitionSpec as P

ITERS = 2
DIMS = 64
PIECE = 128
CHUNK = 256
TALL = 512
WIDE = 512
HALF = 4
BLOCK = 8
STACK = 3 * DIMS + 16
SAMPLES = 32768

Z_GROUPS = [[4 * x + z for z in range(4)] for x in range(4)]
YC_GROUPS = [list(range(8)), list(range(8, 16))]
SHIFTS = (1, 3, 2)


def nn(a, b):
    return lax.dot_general(a, b, (((1,), (0,)), ((), ())), preferred_element_type=jnp.float32)


def tile_kernel(
    where_ref, values_ref, r0, r1, r2, r3, cols_ref, o0, o1, o2, o3, cols_out,
    left, right, stack, table, norm_i, norm_j, acc, acc_lead,
):
    step = pl.program_id(0)
    lead_base, trail_base, diagonal = where_ref[0], where_ref[1], where_ref[2]
    x_pos, z_pos = where_ref[3], where_ref[4]

    def at(n, length=CHUNK):
        return pl.ds(pl.multiple_of(n * CHUNK, CHUNK), length)

    def chunks(row_refs, col_ref, send):
        for ref, shift in zip(row_refs, (0, *SHIFTS)):
            group = lax.rem(x_pos + (shift if send else 4 - shift), 4)
            for m in range(2):
                yield 2 * group + m, ref.at[2 * m], ref.at[2 * m + 1]
        for s in range(2):
            half = z_pos if s == 0 else 1 - z_pos
            for m in range(4):
                yield BLOCK + 4 * half + m, col_ref.at[2 * m, s], col_ref.at[2 * m + 1, s]

    inputs = lambda: chunks((r0, r1, r2, r3), cols_ref, False)

    @pl.when(step == 0)
    def _():
        acc[...] = jnp.zeros_like(acc)
        acc_lead[...] = jnp.zeros_like(acc_lead)
        ones = jnp.ones((16, CHUNK), jnp.bfloat16)
        for n, a, b in inputs():
            x = jnp.concatenate([a[...], b[...]], axis=1)
            hi = x.astype(jnp.bfloat16)
            hi32 = hi.astype(jnp.float32)
            rest = x - hi32
            mid = rest.astype(jnp.bfloat16)
            mid32 = mid.astype(jnp.float32)
            lo = (rest - mid32).astype(jnp.bfloat16)
            stack[:, at(n)] = jnp.concatenate([hi, mid, lo, ones], axis=0)
            right[:, at(n)] = -2.0 * jnp.concatenate([hi, mid, mid, hi], axis=0)
            main = jnp.concatenate([hi32, mid32], axis=0).T.astype(jnp.bfloat16)
            tail = jnp.concatenate([lo.astype(jnp.float32), jnp.ones_like(x)], axis=0).T.astype(jnp.bfloat16)
            left[at(n), :] = jnp.concatenate([main, main], axis=1)
            table[at(n), :] = jnp.concatenate([main, tail], axis=1)
            near = hi32 + mid32
            norms = jnp.sum(near * near, axis=0, keepdims=True)
            norm_j[:, at(n)] = jnp.broadcast_to(norms + 1.0, (8, CHUNK))
            norm_i[at(n), :] = jnp.broadcast_to(norms, (PIECE, CHUNK)).T

    def ratios_of(values, lead, trail):
        inner = nn(left[at(lead, values.shape[0]), :], right[:, at(trail, values.shape[1])])
        ni = jnp.concatenate([norm_i[at(lead, values.shape[0]), :]] * (values.shape[1] // PIECE), axis=1)
        squared = inner + (ni + norm_j[0:1, at(trail, values.shape[1])])
        return values * lax.rsqrt(squared)

    def products(ratios, lead, trail):
        tall, wide = ratios.shape
        hi = ratios.astype(jnp.bfloat16)
        lo = (ratios - hi.astype(jnp.float32)).astype(jnp.bfloat16)
        above, beside = stack[:, at(lead, tall)], table[at(trail, wide), :]
        acc[:, at(trail, wide)] += nn(above, hi) + nn(above, lo)
        acc_lead[at(lead - lead_base, tall), :] += nn(hi, beside) + nn(lo, beside)

    special = jnp.logical_and(diagonal == 1, step < 2)

    @pl.when(jnp.logical_not(special))
    def _():
        lead = lead_base + 2 * step
        for j in range(0, 1024, WIDE):
            trail = trail_base + j // CHUNK
            products(ratios_of(values_ref[:, j : j + WIDE], lead, trail), lead, trail)

    @pl.when(special)
    def _():
        row_iota = lax.broadcasted_iota(jnp.int32, (CHUNK, CHUNK), 0)
        col_iota = lax.broadcasted_iota(jnp.int32, (CHUNK, CHUNK), 1)
        for i in range(2):
            here = 2 * step + i
            for j in range(HALF):
                values = values_ref[i * CHUNK : (i + 1) * CHUNK, j * CHUNK : (j + 1) * CHUNK]

                @pl.when(here != j)
                def _():
                    shift = jnp.where(here > j, HALF, 0)
                    products(ratios_of(values, here + shift, j + shift), here + shift, j + shift)

                @pl.when(here == j)
                def _():
                    for shift, keep in ((0, col_iota > row_iota), (HALF, col_iota < row_iota)):
                        ratios = jnp.where(keep, ratios_of(values, j + shift, j + shift), 0.0)
                        products(ratios, j + shift, j + shift)

    @pl.when(step == pl.num_programs(0) - 1)
    def _():
        for n in range(BLOCK):
            acc[:, at(lead_base + n)] += acc_lead[n * CHUNK : (n + 1) * CHUNK, :].T[:STACK]

        def terms_of(n, a, b):
            x = jnp.concatenate([a[...], b[...]], axis=1)
            part = acc[:, at(n)]
            pulled = part[0:DIMS] + part[DIMS : 2 * DIMS] + part[2 * DIMS : 3 * DIMS]
            return x * part[3 * DIMS : 3 * DIMS + 1] - pulled

        by_send = ((r0, o0), (r2, o1), (r1, o2), (r3, o3))
        sources = list(chunks([a for a, _ in by_send], cols_ref, True))
        targets = list(chunks([b for _, b in by_send], cols_out, True))
        for (n, a, b), (_, c, d) in zip(sources, targets):
            terms = terms_of(n, a, b)
            c[...] = terms[:, :PIECE]
            d[...] = terms[:, PIECE:]


def tile_terms(where, values, groups, cols):
    row_shape = jax.ShapeDtypeStruct(groups[0].shape, jnp.float32)
    col_shape = jax.ShapeDtypeStruct(cols.shape, jnp.float32)
    row_spec = pl.BlockSpec(row_shape.shape, lambda i, w: (0, 0, 0))
    col_spec = pl.BlockSpec(col_shape.shape, lambda i, w: (0, 0, 0, 0))
    total = 2 * BLOCK * CHUNK
    return pl.pallas_call(
        tile_kernel,
        out_shape=(row_shape,) * 4 + (col_shape,),
        grid_spec=pltpu.PrefetchScalarGridSpec(
            num_scalar_prefetch=1,
            grid=(values.shape[0] // TALL,),
            in_specs=[pl.BlockSpec((TALL, values.shape[1]), lambda i, w: (i, 0))] + [row_spec] * 4 + [col_spec],
            out_specs=(row_spec,) * 4 + (col_spec,),
            scratch_shapes=[
                pltpu.VMEM((total, CHUNK), jnp.bfloat16),
                pltpu.VMEM((CHUNK, total), jnp.bfloat16),
                pltpu.VMEM((STACK, total), jnp.bfloat16),
                pltpu.VMEM((total, CHUNK), jnp.bfloat16),
                pltpu.VMEM((total, PIECE), jnp.float32),
                pltpu.VMEM((8, total), jnp.float32),
                pltpu.VMEM((STACK, total), jnp.float32),
                pltpu.VMEM((total // 2, CHUNK), jnp.float32),
            ],
        ),
        compiler_params=pltpu.CompilerParams(
            dimension_semantics=("arbitrary",), vmem_limit_bytes=56 * 1024 * 1024
        ),
        cost_estimate=pl.CostEstimate(flops=6_000_000_000, transcendentals=2_097_152, bytes_accessed=10_000_000),
    )(where, values, *groups, cols)


def exchange(x, axis, groups):
    return lax.all_to_all(x, axis, split_axis=0, concat_axis=0, tiled=True, axis_index_groups=groups)


def spread(x, axis, groups):
    return exchange(jnp.broadcast_to(x, (len(groups[0]), *x.shape)), axis, groups)


def transposed(x):
    pairs = [(a * 16 + b, b * 16 + a) for a in range(16) for b in range(16)]
    return lax.ppermute(x, ("row", "col"), pairs)


def across(x):
    return lax.ppermute(x, "row", [(a, (a + 8) % 16) for a in range(16)])


def along(x, shift):
    return lax.ppermute(x, "col", [(a, (a + 4 * shift) % 16) for a in range(16)])


def gathered(own, turned):
    line = spread(own, "col", Z_GROUPS)
    other = across(turned)
    cols = spread(jnp.stack([turned, other]), "row", YC_GROUPS)
    return (line, *(along(line, s) for s in SHIFTS)), cols


def reduced(groups, cols):
    kept, sent = exchange(cols, "row", YC_GROUPS).sum(axis=0)
    line = groups[0]
    for part, s in zip(groups[1:], SHIFTS):
        line = line + along(part, s)
    came = across(sent)
    row_sum = exchange(line, "col", Z_GROUPS).sum(axis=0)
    return row_sum, kept + came


def local(coords, dissimilarity):
    row, col = lax.axis_index("row"), lax.axis_index("col")
    lead_base = jnp.where(row > col, BLOCK, 0)
    trail_base = jnp.where(row < col, BLOCK, jnp.where(row > col, HALF, 0))
    diagonal = (row == col).astype(jnp.int32)
    where = jnp.stack([lead_base, trail_base, diagonal, col // 4, row // 8]).astype(jnp.int32)
    own, turned = coords, transposed(coords)
    scale = 1.0 / SAMPLES
    for iteration in range(ITERS):
        groups, cols = gathered(own, turned)
        *groups, cols = tile_terms(where, dissimilarity, groups, cols)
        row_sum, col_sum = reduced(groups, cols)
        if iteration + 1 < ITERS:
            came = transposed(jnp.stack([row_sum, col_sum]))
            own = (row_sum + came[1]) * scale
            turned = (col_sum + came[0]) * scale
        else:
            own = (row_sum + transposed(col_sum)) * scale
    return own


def solution(mesh):
    in_specs = (P(None, ("row", "col")), P("row", "col"))
    out_specs = P(None, ("row", "col"))
    return jax.shard_map(local, mesh=mesh, in_specs=in_specs, out_specs=out_specs, check_vma=False)
```

```python
import jax
import jax.numpy as jnp
from jax import lax
from jax.experimental import pallas as pl
from jax.experimental.pallas import tpu as pltpu
from jax.sharding import PartitionSpec as P

ITERS = 2
DIMS = 64
PIECE = 128
CHUNK = 256
TALL = 512
WIDE = 512
HALF = 4
STEPS = 4
BLOCK = 8
STACK = 3 * DIMS + 16
SAMPLES = 32768

Z_GROUPS = [[4 * x + z for z in range(4)] for x in range(4)]
YC_GROUPS = [list(range(8)), list(range(8, 16))]
SHIFTS = (1, 3, 2)


def nn(a, b):
    return lax.dot_general(a, b, (((1,), (0,)), ((), ())), preferred_element_type=jnp.float32)


def tile_kernel(
    where_ref, values_hbm, *refs,
):
    sources, targets = refs[:5], refs[5:10]
    (given, made), (given_cols, made_cols) = refs[10:12], refs[12:14]
    values_ref, left, right, stack, table, norm_i, norm_j, acc, acc_lead, value_sem, coord_sem, term_sem = refs[14:]
    lead_base, trail_base, diagonal = where_ref[0], where_ref[1], where_ref[2]
    x_pos, z_pos = where_ref[3], where_ref[4]

    def at(n, length=CHUNK):
        return pl.ds(pl.multiple_of(n * CHUNK, CHUNK), length)

    def band(step):
        return pl.ds(pl.multiple_of(step * TALL, TALL), TALL)

    def value_copy(step):
        return pltpu.make_async_copy(values_hbm.at[band(step)], values_ref.at[band(step)], value_sem.at[step])

    def row_group(t, send):
        shift = (0, *SHIFTS)[t]
        return lax.rem(x_pos + (shift if send else 4 - shift), 4)

    coord_copies = [pltpu.make_async_copy(sources[t], given.at[row_group(t, False)], coord_sem.at[t]) for t in range(4)]
    coord_copies.append(pltpu.make_async_copy(sources[4], given_cols, coord_sem.at[4]))
    term_copies = [pltpu.make_async_copy(made.at[row_group(t, True)], targets[t], term_sem.at[t]) for t in range(4)]
    term_copies.append(pltpu.make_async_copy(made_cols, targets[4], term_sem.at[4]))

    for copy in coord_copies:
        copy.start()
    for step in range(STEPS):
        value_copy(step).start()
    acc[...] = jnp.zeros_like(acc)
    acc_lead[...] = jnp.zeros_like(acc_lead)
    for copy in coord_copies:
        copy.wait()

    def places():
        for n in range(BLOCK):
            yield n, given.at[n // 2, n % 2 * 2], given.at[n // 2, n % 2 * 2 + 1], made.at[n // 2, n % 2 * 2], made.at[n // 2, n % 2 * 2 + 1]
        for s in range(2):
            half = z_pos if s == 0 else 1 - z_pos
            for m in range(4):
                n = BLOCK + 4 * half + m
                yield n, given_cols.at[2 * m, s], given_cols.at[2 * m + 1, s], made_cols.at[2 * m, s], made_cols.at[2 * m + 1, s]

    for n, a, b, _, _ in places():
        def split():
            x = jnp.concatenate([a[...], b[...]], axis=1)
            hi = x.astype(jnp.bfloat16)
            hi32 = hi.astype(jnp.float32)
            rest = x - hi32
            mid = rest.astype(jnp.bfloat16)
            mid32 = mid.astype(jnp.float32)
            lo = (rest - mid32).astype(jnp.bfloat16)
            near = hi32 + mid32
            norms = jnp.sum(near * near, axis=0, keepdims=True)
            main = jnp.concatenate([hi32, mid32], axis=0).T.astype(jnp.bfloat16)
            return hi, mid, lo, norms, main

        @pl.when(jnp.logical_and(n >= lead_base, n < lead_base + BLOCK))
        def _():
            hi, mid, lo, norms, main = split()
            stack[:, at(n)] = jnp.concatenate([hi, mid, lo, jnp.ones((16, CHUNK), jnp.bfloat16)], axis=0)
            left[at(n), :] = jnp.concatenate([main, main], axis=1)
            norm_i[at(n), :] = jnp.broadcast_to(norms, (PIECE, CHUNK)).T

        @pl.when(jnp.logical_and(n >= trail_base, n < trail_base + jnp.where(diagonal == 1, BLOCK, HALF)))
        def _():
            hi, mid, lo, norms, main = split()
            right[:, at(n)] = -2.0 * jnp.concatenate([hi, mid, mid, hi], axis=0)
            lo32 = lo.astype(jnp.float32)
            tail = jnp.concatenate([lo32, jnp.ones_like(lo32)], axis=0).T.astype(jnp.bfloat16)
            table[at(n), :] = jnp.concatenate([main, tail], axis=1)
            norm_j[:, at(n)] = jnp.broadcast_to(norms + 1.0, (8, CHUNK))

    def ratios_of(values, lead, trail):
        inner = nn(left[at(lead, TALL), :], right[:, at(trail, WIDE)])
        ni = jnp.concatenate([norm_i[at(lead, TALL), :]] * (WIDE // PIECE), axis=1)
        squared = inner + (ni + norm_j[0:1, at(trail, WIDE)])
        return values * lax.rsqrt(squared)

    def products(ratios, lead, trail):
        hi = ratios.astype(jnp.bfloat16)
        lo = (ratios - hi.astype(jnp.float32)).astype(jnp.bfloat16)
        above, beside = stack[:, at(lead, TALL)], table[at(trail, WIDE), :]
        acc[:, at(trail, WIDE)] += nn(above, hi) + nn(above, lo)
        acc_lead[at(lead - lead_base, TALL), :] += nn(hi, beside) + nn(lo, beside)

    def values_at(step, j):
        return values_ref[band(step), pl.ds(pl.multiple_of(j * WIDE, WIDE), WIDE)]

    @pl.loop(0, STEPS)
    def _(step):
        value_copy(step).wait()
        special = jnp.logical_and(diagonal == 1, step < 2)

        @pl.when(jnp.logical_not(special))
        def _():
            lead = lead_base + 2 * step
            for j in range(2):
                trail = trail_base + 2 * j
                products(ratios_of(values_at(step, j), lead, trail), lead, trail)

        @pl.when(special)
        def _():
            @pl.loop(0, 3)
            def _(k):
                late = jnp.logical_or(k == 2, jnp.logical_and(step == 1, k == 1)).astype(jnp.int32)
                j = jnp.where(step == 0, k % 2, jnp.where(k == 1, 0, 1))
                row_iota = lax.broadcasted_iota(jnp.int32, (TALL, WIDE), 0) + step * TALL
                col_iota = lax.broadcasted_iota(jnp.int32, (TALL, WIDE), 1) + j * WIDE
                keep = (col_iota - row_iota) * (1 - 2 * late) > 0
                lead, trail = 2 * step + HALF * late, 2 * j + HALF * late
                ratios = jnp.where(keep, ratios_of(values_at(step, j), lead, trail), 0.0)
                products(ratios, lead, trail)

    for n in range(BLOCK):
        acc[:, at(lead_base + n)] += acc_lead[n * CHUNK : (n + 1) * CHUNK, :].T[:STACK]
    for k, (n, a, b, c, d) in enumerate(places()):
        x = jnp.concatenate([a[...], b[...]], axis=1)
        part = acc[:, at(n)]
        pulled = part[0:DIMS] + part[DIMS : 2 * DIMS] + part[2 * DIMS : 3 * DIMS]
        terms = x * part[3 * DIMS : 3 * DIMS + 1] - pulled
        c[...] = terms[:, :PIECE]
        d[...] = terms[:, PIECE:]
        if k == BLOCK - 1:
            for copy in term_copies[:4]:
                copy.start()
    term_copies[4].start()
    for copy in term_copies:
        copy.wait()


def tile_terms(where, values, groups, cols):
    row_shape = jax.ShapeDtypeStruct(groups[0].shape, jnp.float32)
    col_shape = jax.ShapeDtypeStruct(cols.shape, jnp.float32)
    total = 2 * BLOCK * CHUNK
    anywhere = pl.BlockSpec(memory_space=pl.ANY)
    rows_buffer = pltpu.VMEM((4, *groups[0].shape), jnp.float32)
    cols_buffer = pltpu.VMEM(cols.shape, jnp.float32)
    return pl.pallas_call(
        tile_kernel,
        out_shape=(row_shape,) * 4 + (col_shape,),
        in_specs=[pl.BlockSpec(memory_space=pltpu.SMEM)] + [anywhere] * 6,
        out_specs=(anywhere,) * 5,
        scratch_shapes=[
            rows_buffer, rows_buffer, cols_buffer, cols_buffer,
            pltpu.VMEM(values.shape, jnp.float32),
            pltpu.VMEM((total, CHUNK), jnp.bfloat16),
            pltpu.VMEM((CHUNK, total), jnp.bfloat16),
            pltpu.VMEM((STACK, total), jnp.bfloat16),
            pltpu.VMEM((total, CHUNK), jnp.bfloat16),
            pltpu.VMEM((total, PIECE), jnp.float32),
            pltpu.VMEM((8, total), jnp.float32),
            pltpu.VMEM((STACK, total), jnp.float32),
            pltpu.VMEM((total // 2, CHUNK), jnp.float32),
            pltpu.SemaphoreType.DMA((STEPS,)),
            pltpu.SemaphoreType.DMA((5,)),
            pltpu.SemaphoreType.DMA((5,)),
        ],
        compiler_params=pltpu.CompilerParams(vmem_limit_bytes=48 * 1024 * 1024),
        cost_estimate=pl.CostEstimate(flops=6_000_000_000, transcendentals=2_097_152, bytes_accessed=10_000_000),
    )(where, values, *groups, cols)


def exchange(x, axis, groups):
    return lax.all_to_all(x, axis, split_axis=0, concat_axis=0, tiled=True, axis_index_groups=groups)


def spread(x, axis, groups):
    return exchange(jnp.broadcast_to(x, (len(groups[0]), *x.shape)), axis, groups)


def transposed(x):
    pairs = [(a * 16 + b, b * 16 + a) for a in range(16) for b in range(16)]
    return lax.ppermute(x, ("row", "col"), pairs)


def across(x):
    return lax.ppermute(x, "row", [(a, (a + 8) % 16) for a in range(16)])


def along(x, shift):
    return lax.ppermute(x, "col", [(a, (a + 4 * shift) % 16) for a in range(16)])


def gathered(own, turned):
    line = spread(own, "col", Z_GROUPS)
    other = across(turned)
    cols = spread(jnp.stack([turned, other]), "row", YC_GROUPS)
    return (line, *(along(line, s) for s in SHIFTS)), cols


def reduced(groups, cols):
    kept, sent = exchange(cols, "row", YC_GROUPS).sum(axis=0)
    line = groups[0]
    for part, s in zip(groups[1:], SHIFTS):
        line = line + along(part, s)
    came = across(sent)
    row_sum = exchange(line, "col", Z_GROUPS).sum(axis=0)
    return row_sum, kept + came


def local(coords, dissimilarity):
    row, col = lax.axis_index("row"), lax.axis_index("col")
    lead_base = jnp.where(row > col, BLOCK, 0)
    trail_base = jnp.where(row < col, BLOCK, jnp.where(row > col, HALF, 0))
    diagonal = (row == col).astype(jnp.int32)
    where = jnp.stack([lead_base, trail_base, diagonal, col // 4, row // 8]).astype(jnp.int32)
    own, turned = coords, transposed(coords)
    scale = 1.0 / SAMPLES
    for iteration in range(ITERS):
        groups, cols = gathered(own, turned)
        *groups, cols = tile_terms(where, dissimilarity, groups, cols)
        row_sum, col_sum = reduced(groups, cols)
        if iteration + 1 < ITERS:
            came = transposed(jnp.stack([row_sum, col_sum]))
            own = (row_sum + came[1]) * scale
            turned = (col_sum + came[0]) * scale
        else:
            own = (row_sum + transposed(col_sum)) * scale
    return own


def solution(mesh):
    in_specs = (P(None, ("row", "col")), P("row", "col"))
    out_specs = P(None, ("row", "col"))
    return jax.shard_map(local, mesh=mesh, in_specs=in_specs, out_specs=out_specs, check_vma=False)
```

```python
import jax
import jax.numpy as jnp
from jax import lax
from jax.experimental import pallas as pl
from jax.experimental.pallas import tpu as pltpu
from jax.sharding import PartitionSpec as P

ITERS = 2
DIMS = 64
PIECE = 128
CHUNK = 256
TALL = 512
WIDE = 512
HALF = 4
STEPS = 4
BLOCK = 8
STACK = 3 * DIMS + 16
SAMPLES = 32768

SHIFTS = (1, 3, 2)


def nn(a, b):
    return lax.dot_general(a, b, (((1,), (0,)), ((), ())), preferred_element_type=jnp.float32)


def tile_kernel(where_ref, values_hbm, *refs):
    sources, targets = refs[:9], refs[9:18]
    given, made, values_ref, left, right, stack, table, norm_i, norm_j, acc, acc_lead = refs[18:29]
    value_sem, coord_sem, term_sem = refs[29:]
    lead_base, trail_base, diagonal = where_ref[0], where_ref[1], where_ref[2]
    x_pos, line_pos, half_pos, y_pos, core = (where_ref[k] for k in range(3, 8))

    def at(n, length=CHUNK):
        return pl.ds(pl.multiple_of(n * CHUNK, CHUNK), length)

    def band(step):
        return pl.ds(pl.multiple_of(step * TALL, TALL), TALL)

    def value_copy(step):
        return pltpu.make_async_copy(values_hbm.at[band(step)], values_ref.at[band(step)], value_sem.at[step])

    def places(refs, send):
        for t, shift in enumerate((0, *SHIFTS)):
            group = lax.rem(x_pos + (shift if send else 4 - shift), 4)
            for i in range(4):
                line = lax.bitwise_xor(line_pos, i)
                yield 4 * group + line, refs[t].at[i]
        for t, shift in enumerate((0, *SHIFTS)):
            y = lax.rem(y_pos + (shift if send else 4 - shift), 4)
            for s in range(2):
                half = half_pos if s == 0 else 1 - half_pos
                yield 16 + 8 * half + 2 * y + core, refs[4 + t].at[s]
                yield 16 + 8 * half + 2 * y + (1 - core), refs[8].at[t, s]

    coord_copies = [
        pltpu.make_async_copy(ref, given.at[n], coord_sem.at[k]) for k, (n, ref) in enumerate(places(sources, False))
    ]
    term_copies = [
        pltpu.make_async_copy(made.at[n], ref, term_sem.at[k]) for k, (n, ref) in enumerate(places(targets, True))
    ]

    for copy in coord_copies:
        copy.start()
    for step in range(STEPS):
        value_copy(step).start()
    acc[...] = jnp.zeros_like(acc)
    acc_lead[...] = jnp.zeros_like(acc_lead)
    for copy in coord_copies:
        copy.wait()

    def coords_of(n):
        return jnp.concatenate([given[2 * n], given[2 * n + 1]], axis=1)

    def split(n):
        x = coords_of(n)
        hi = x.astype(jnp.bfloat16)
        hi32 = hi.astype(jnp.float32)
        rest = x - hi32
        mid = rest.astype(jnp.bfloat16)
        mid32 = mid.astype(jnp.float32)
        lo = (rest - mid32).astype(jnp.bfloat16)
        near = hi32 + mid32
        norms = jnp.sum(near * near, axis=0, keepdims=True)
        main = jnp.concatenate([hi32, mid32], axis=0).T.astype(jnp.bfloat16)
        return hi, mid, lo, norms, main

    for k in range(BLOCK):
        n = lead_base + k
        hi, mid, lo, norms, main = split(n)
        stack[:, at(k)] = jnp.concatenate([hi, mid, lo, jnp.ones((16, CHUNK), jnp.bfloat16)], axis=0)
        left[at(k), :] = jnp.concatenate([main, main], axis=1)
        norm_i[at(k), :] = jnp.broadcast_to(norms, (PIECE, CHUNK)).T

    def trail_chunk(n):
        hi, mid, lo, norms, main = split(n)
        right[:, at(n)] = -2.0 * jnp.concatenate([hi, mid, mid, hi], axis=0)
        lo32 = lo.astype(jnp.float32)
        tail = jnp.concatenate([lo32, jnp.ones_like(lo32)], axis=0).T.astype(jnp.bfloat16)
        table[at(n), :] = jnp.concatenate([main, tail], axis=1)
        norm_j[:, at(n)] = jnp.broadcast_to(norms + 1.0, (8, CHUNK))

    for k in range(HALF):
        trail_chunk(trail_base + k)

    @pl.when(diagonal == 1)
    def _():
        @pl.loop(HALF, BLOCK)
        def _(k):
            trail_chunk(k)

    def ratios_of(values, lead, trail):
        inner = nn(left[at(lead - lead_base, TALL), :], right[:, at(trail, WIDE)])
        ni = jnp.concatenate([norm_i[at(lead - lead_base, TALL), :]] * (WIDE // PIECE), axis=1)
        squared = inner + (ni + norm_j[0:1, at(trail, WIDE)])
        return values * lax.rsqrt(squared)

    def products(ratios, lead, trail):
        hi = ratios.astype(jnp.bfloat16)
        lo = (ratios - hi.astype(jnp.float32)).astype(jnp.bfloat16)
        above, beside = stack[:, at(lead - lead_base, TALL)], table[at(trail, WIDE), :]
        acc[:, at(trail, WIDE)] += nn(above, hi) + nn(above, lo)
        acc_lead[at(lead - lead_base, TALL), :] += nn(hi, beside) + nn(lo, beside)

    def values_at(step, j):
        return values_ref[band(step), pl.ds(pl.multiple_of(j * WIDE, WIDE), WIDE)]

    @pl.loop(0, STEPS)
    def _(step):
        value_copy(step).wait()
        special = jnp.logical_and(diagonal == 1, step < 2)

        @pl.when(jnp.logical_not(special))
        def _():
            lead = lead_base + 2 * step
            for j in range(2):
                trail = trail_base + 2 * j
                products(ratios_of(values_at(step, j), lead, trail), lead, trail)

        @pl.when(special)
        def _():
            @pl.loop(0, 3)
            def _(k):
                late = jnp.logical_or(k == 2, jnp.logical_and(step == 1, k == 1)).astype(jnp.int32)
                j = jnp.where(step == 0, k % 2, jnp.where(k == 1, 0, 1))
                row_iota = lax.broadcasted_iota(jnp.int32, (TALL, WIDE), 0) + step * TALL
                col_iota = lax.broadcasted_iota(jnp.int32, (TALL, WIDE), 1) + j * WIDE
                keep = (col_iota - row_iota) * (1 - 2 * late) > 0
                lead, trail = 2 * step + HALF * late, 2 * j + HALF * late
                ratios = jnp.where(keep, ratios_of(values_at(step, j), lead, trail), 0.0)
                products(ratios, lead, trail)

    for n in range(BLOCK):
        acc[:, at(lead_base + n)] += acc_lead[n * CHUNK : (n + 1) * CHUNK, :].T[:STACK]
    for n in range(2 * BLOCK):
        part = acc[:, at(n)]
        pulled = part[0:DIMS] + part[DIMS : 2 * DIMS] + part[2 * DIMS : 3 * DIMS]
        terms = coords_of(n) * part[3 * DIMS : 3 * DIMS + 1] - pulled
        made[2 * n] = terms[:, :PIECE]
        made[2 * n + 1] = terms[:, PIECE:]
        if n == BLOCK - 1:
            for copy in term_copies[:16]:
                copy.start()
    for copy in term_copies[16:]:
        copy.start()
    for copy in term_copies:
        copy.wait()


def tile_terms(where, values, *coords):
    shapes = tuple(jax.ShapeDtypeStruct(x.shape, jnp.float32) for x in coords)
    total = 2 * BLOCK * CHUNK
    anywhere = pl.BlockSpec(memory_space=pl.ANY)
    pieces = pltpu.VMEM((32, DIMS, PIECE), jnp.float32)
    return pl.pallas_call(
        tile_kernel,
        out_shape=shapes,
        in_specs=[pl.BlockSpec(memory_space=pltpu.SMEM)] + [anywhere] * (1 + len(coords)),
        out_specs=(anywhere,) * len(coords),
        scratch_shapes=[
            pieces,
            pieces,
            pltpu.VMEM(values.shape, jnp.float32),
            pltpu.VMEM((total // 2, CHUNK), jnp.bfloat16),
            pltpu.VMEM((CHUNK, total), jnp.bfloat16),
            pltpu.VMEM((STACK, total // 2), jnp.bfloat16),
            pltpu.VMEM((total, CHUNK), jnp.bfloat16),
            pltpu.VMEM((total // 2, PIECE), jnp.float32),
            pltpu.VMEM((8, total), jnp.float32),
            pltpu.VMEM((STACK, total), jnp.float32),
            pltpu.VMEM((total // 2, CHUNK), jnp.float32),
            pltpu.SemaphoreType.DMA((STEPS,)),
            pltpu.SemaphoreType.DMA((32,)),
            pltpu.SemaphoreType.DMA((32,)),
        ],
        compiler_params=pltpu.CompilerParams(vmem_limit_bytes=48 * 1024 * 1024),
        cost_estimate=pl.CostEstimate(flops=6_000_000_000, transcendentals=2_097_152, bytes_accessed=10_000_000),
    )(where, values, *coords)


def transposed(x, before=0, after=0):
    pairs = [(a * 16 + b, (b ^ after) * 16 + (a ^ before)) for a in range(16) for b in range(16)]
    return lax.ppermute(x, ("row", "col"), pairs)


def across(x):
    return lax.ppermute(x, "row", [(a, (a + 8) % 16) for a in range(16)])


def along_x(x, shift):
    return lax.ppermute(x, "col", [(a, (a + 4 * shift) % 16) for a in range(16)])


def along_y(x, shift):
    return lax.ppermute(x, "row", [(a, a // 8 * 8 + (a + 2 * shift) % 8) for a in range(16)])


def along_z(x, flip):
    return lax.ppermute(x, "col", [(a, a ^ flip) for a in range(16)])


def swapped(x):
    return lax.ppermute(x, "row", [(a, a ^ 1) for a in range(16)])


def gathered(own, both):
    line = jnp.stack([own, *(along_z(own, f) for f in (1, 2, 3))])
    line, both = lax.optimization_barrier((line, both))
    groups = [along_x(line, s) for s in SHIFTS]
    cols = (both, *(along_y(both, s) for s in SHIFTS))
    twin = jnp.stack(cols)
    *groups, twin = lax.optimization_barrier((*groups, twin))
    return line, *groups, *cols, swapped(twin)


def reduced(*parts):
    rows, cols, twin = parts[:4], parts[4:8], swapped(parts[8])
    line = rows[0]
    for part, s in zip(rows[1:], SHIFTS):
        line = line + along_x(part, s)
    mine = [c + t for c, t in zip(cols, twin)]
    total = mine[0]
    for part, s in zip(mine[1:], SHIFTS):
        total = total + along_y(part, s)
    row_sum = line[0]
    for f in (1, 2, 3):
        row_sum = row_sum + along_z(line[f], f)
    return row_sum, total


def local(coords, dissimilarity):
    row, col = lax.axis_index("row"), lax.axis_index("col")
    lead_base = jnp.where(row > col, BLOCK, 0)
    trail_base = jnp.where(row < col, BLOCK, jnp.where(row > col, HALF, 0))
    diagonal = (row == col).astype(jnp.int32)
    place = [col // 4, col % 4, row // 8, row // 2 % 4, row % 2]
    where = jnp.stack([lead_base, trail_base, diagonal, *place]).astype(jnp.int32)
    scale = 1.0 / SAMPLES
    own = coords
    both = jnp.stack([transposed(coords), transposed(coords, after=8)])
    for iteration in range(ITERS):
        parts = tile_terms(where, dissimilarity, *gathered(own, both))
        row_sum, total = reduced(*parts)
        if iteration + 1 < ITERS:
            col_sum = total[0] + across(total[1])
            came = transposed(jnp.stack([row_sum, col_sum]))
            own = (row_sum + came[1]) * scale
            turned = (col_sum + came[0]) * scale
            both = jnp.stack([turned, across(turned)])
        else:
            own = (row_sum + transposed(total[0]) + transposed(total[1], before=8)) * scale
    return own


def solution(mesh):
    in_specs = (P(None, ("row", "col")), P("row", "col"))
    out_specs = P(None, ("row", "col"))
    return jax.shard_map(local, mesh=mesh, in_specs=in_specs, out_specs=out_specs, check_vma=False)
```

```python
import jax
import jax.numpy as jnp
import numpy as np
from jax import lax
from jax.experimental import pallas as pl
from jax.experimental.pallas import tpu as pltpu
from jax.sharding import PartitionSpec as P

ITERS = 2
DIMS = 64
PIECE = 128
CHUNK = 256
TALL = 512
WIDE = 512
HALF = 4
STEPS = 4
BLOCK = 8
STACK = 3 * DIMS + 16
HEAD = 6
SAMPLES = 32768

SHIFTS = (1, 3, 2)


def nn(a, b):
    return lax.dot_general(a, b, (((1,), (0,)), ((), ())), preferred_element_type=jnp.float32)


def tile_kernel(where_ref, values_hbm, *refs):
    sources, targets = refs[:9], refs[9:18]
    given, made, values_ref, left, right, stack, table, norm_i, norm_j, acc, acc_lead = refs[18:29]
    value_sem, coord_sem, term_sem = refs[29:]
    lead_base, trail_base, diagonal = where_ref[0], where_ref[1], where_ref[2]
    x_pos, y_pos, core = where_ref[3], where_ref[4], where_ref[5]

    def at(n, length=CHUNK):
        return pl.ds(pl.multiple_of(n * CHUNK, CHUNK), length)

    def band(step):
        return pl.ds(pl.multiple_of(step * TALL, TALL), TALL)

    def value_copy(step):
        return pltpu.make_async_copy(values_hbm.at[band(step)], values_ref.at[band(step)], value_sem.at[step])

    def moves(refs, send):
        for t, shift in enumerate((0, *SHIFTS)):
            group = lax.rem(x_pos + (shift if send else 4 - shift), 4)
            yield pl.ds(4 * group, 4), refs[t]
        for t, shift in enumerate((0, *SHIFTS)):
            y = lax.rem(y_pos + (shift if send else 4 - shift), 4)
            yield pl.ds(16 + 8 * core + 2 * y, 2), refs[4 + t]
            yield pl.ds(16 + 8 * (1 - core) + 2 * y, 2), refs[8].at[t]

    coord_copies = [
        pltpu.make_async_copy(ref, given.at[slots], coord_sem.at[k]) for k, (slots, ref) in enumerate(moves(sources, False))
    ]
    term_copies = [
        pltpu.make_async_copy(made.at[slots], ref, term_sem.at[k]) for k, (slots, ref) in enumerate(moves(targets, True))
    ]

    for copy in coord_copies:
        copy.start()
    for step in range(STEPS):
        value_copy(step).start()
    acc[...] = jnp.zeros_like(acc)
    acc_lead[...] = jnp.zeros_like(acc_lead)
    for copy in coord_copies:
        copy.wait()

    def coords_of(n):
        return jnp.concatenate([given[where_ref[HEAD + 2 * n]], given[where_ref[HEAD + 2 * n + 1]]], axis=1)

    def split(n):
        x = coords_of(n)
        hi = x.astype(jnp.bfloat16)
        hi32 = hi.astype(jnp.float32)
        rest = x - hi32
        mid = rest.astype(jnp.bfloat16)
        mid32 = mid.astype(jnp.float32)
        lo = (rest - mid32).astype(jnp.bfloat16)
        near = hi32 + mid32
        norms = jnp.sum(near * near, axis=0, keepdims=True)
        main = jnp.concatenate([hi32, mid32], axis=0).T.astype(jnp.bfloat16)
        return hi, mid, lo, norms, main

    for k in range(BLOCK):
        n = lead_base + k
        hi, mid, lo, norms, main = split(n)
        stack[:, at(k)] = jnp.concatenate([hi, mid, lo, jnp.ones((16, CHUNK), jnp.bfloat16)], axis=0)
        left[at(k), :] = jnp.concatenate([main, main], axis=1)
        norm_i[at(k), :] = jnp.broadcast_to(norms, (PIECE, CHUNK)).T

    def trail_chunk(n):
        hi, mid, lo, norms, main = split(n)
        right[:, at(n)] = -2.0 * jnp.concatenate([hi, mid, mid, hi], axis=0)
        lo32 = lo.astype(jnp.float32)
        tail = jnp.concatenate([lo32, jnp.ones_like(lo32)], axis=0).T.astype(jnp.bfloat16)
        table[at(n), :] = jnp.concatenate([main, tail], axis=1)
        norm_j[:, at(n)] = jnp.broadcast_to(norms + 1.0, (8, CHUNK))

    for k in range(HALF):
        trail_chunk(trail_base + k)

    @pl.when(diagonal == 1)
    def _():
        @pl.loop(HALF, BLOCK)
        def _(k):
            trail_chunk(k)

    def ratios_of(values, lead, trail):
        inner = nn(left[at(lead - lead_base, TALL), :], right[:, at(trail, WIDE)])
        ni = jnp.concatenate([norm_i[at(lead - lead_base, TALL), :]] * (WIDE // PIECE), axis=1)
        squared = inner + (ni + norm_j[0:1, at(trail, WIDE)])
        return values * lax.rsqrt(squared)

    def products(ratios, lead, trail):
        hi = ratios.astype(jnp.bfloat16)
        lo = (ratios - hi.astype(jnp.float32)).astype(jnp.bfloat16)
        above, beside = stack[:, at(lead - lead_base, TALL)], table[at(trail, WIDE), :]
        acc[:, at(trail, WIDE)] += nn(above, hi) + nn(above, lo)
        acc_lead[at(lead - lead_base, TALL), :] += nn(hi, beside) + nn(lo, beside)

    def values_at(step, j):
        return values_ref[band(step), j * WIDE : (j + 1) * WIDE]

    @pl.loop(0, STEPS // 2)
    def _(pair):
        value_copy(2 * pair).wait()
        value_copy(2 * pair + 1).wait()
        special = jnp.logical_and(diagonal == 1, pair == 0)

        @pl.when(jnp.logical_not(special))
        def _():
            for i in range(2):
                step = 2 * pair + i
                lead = lead_base + 2 * step
                for j in range(2):
                    trail = trail_base + 2 * j
                    products(ratios_of(values_at(step, j), lead, trail), lead, trail)

        @pl.when(special)
        def _():
            ahead = lax.broadcasted_iota(jnp.int32, (TALL, WIDE), 1) - lax.broadcasted_iota(jnp.int32, (TALL, WIDE), 0)
            for step, j, late in ((0, 0, 0), (0, 1, 0), (0, 0, 1), (1, 1, 0), (1, 0, 1), (1, 1, 1)):
                lead, trail = 2 * step + HALF * late, 2 * j + HALF * late
                ratios = ratios_of(values_at(step, j), lead, trail)
                if step == j:
                    ratios = jnp.where(ahead < 0 if late else ahead > 0, ratios, 0.0)
                products(ratios, lead, trail)

    low_lanes = lax.broadcasted_iota(jnp.int32, (CHUNK, PIECE), 1) < DIMS
    for n in range(BLOCK):
        near, far = acc_lead[n * CHUNK : (n + 1) * CHUNK, :PIECE], acc_lead[n * CHUNK : (n + 1) * CHUNK, PIECE:]
        folded = jnp.where(low_lanes, near + pltpu.roll(near, DIMS, 1) + far, far).T
        acc[:DIMS, at(lead_base + n)] += folded[:DIMS]
        acc[3 * DIMS :, at(lead_base + n)] += folded[DIMS : DIMS + 16]
    for n in range(2 * BLOCK):
        part = acc[:, at(n)]
        pulled = part[0:DIMS] + part[DIMS : 2 * DIMS] + part[2 * DIMS : 3 * DIMS]
        terms = coords_of(n) * part[3 * DIMS : 3 * DIMS + 1] - pulled
        made[where_ref[HEAD + 32 + 2 * n]] = terms[:, :PIECE]
        made[where_ref[HEAD + 33 + 2 * n]] = terms[:, PIECE:]
        if n == BLOCK - 1:
            for copy in term_copies[:4]:
                copy.start()
    for copy in term_copies[4:]:
        copy.start()
    for copy in term_copies:
        copy.wait()


def tile_terms(where, values, *coords):
    shapes = tuple(jax.ShapeDtypeStruct(x.shape, jnp.float32) for x in coords)
    total = 2 * BLOCK * CHUNK
    anywhere = pl.BlockSpec(memory_space=pl.ANY)
    pieces = pltpu.VMEM((32, DIMS, PIECE), jnp.float32)
    return pl.pallas_call(
        tile_kernel,
        out_shape=shapes,
        in_specs=[pl.BlockSpec(memory_space=pltpu.SMEM)] + [anywhere] * (1 + len(coords)),
        out_specs=(anywhere,) * len(coords),
        scratch_shapes=[
            pieces,
            pieces,
            pltpu.VMEM(values.shape, jnp.float32),
            pltpu.VMEM((total // 2, CHUNK), jnp.bfloat16),
            pltpu.VMEM((CHUNK, total), jnp.bfloat16),
            pltpu.VMEM((STACK, total // 2), jnp.bfloat16),
            pltpu.VMEM((total, CHUNK), jnp.bfloat16),
            pltpu.VMEM((total // 2, PIECE), jnp.float32),
            pltpu.VMEM((8, total), jnp.float32),
            pltpu.VMEM((STACK, total), jnp.float32),
            pltpu.VMEM((total // 2, CHUNK), jnp.float32),
            pltpu.SemaphoreType.DMA((STEPS,)),
            pltpu.SemaphoreType.DMA((12,)),
            pltpu.SemaphoreType.DMA((12,)),
        ],
        compiler_params=pltpu.CompilerParams(vmem_limit_bytes=48 * 1024 * 1024),
        cost_estimate=pl.CostEstimate(flops=6_000_000_000, transcendentals=2_097_152, bytes_accessed=10_000_000),
    )(where, values, *coords)


def short_routes():
    def hops(c, p, k):
        def ring(a, b, n):
            return min((a - b) % n, (b - a) % n)

        across_x, across_y = ring(p // 4, c // 4, 4), ring(c // 2 % 4, k // 2 % 4, 4)
        return across_x + across_y + ring(c // 8 * 4 + p % 4, k // 8 * 4 + c % 4, 8)

    def matched(c, pieces, ranks, most):
        taken = {}

        def place(p, seen):
            for k in ranks:
                if k not in seen and hops(c, p, k) <= most:
                    seen.add(k)
                    if k not in taken or place(taken[k], seen):
                        taken[k] = p
                        return True
            return False

        return taken if all(place(p, set()) for p in pieces) else None

    routes, slots = ([], []), np.zeros((2, 16, 16), np.int32)
    for c in range(16):
        even = [p for p in range(16) if (p // 4 + p % 4) % 2 == 0]
        odd = [p for p in range(16) if p not in even]
        for half in range(2):
            ranks = range(8 * half, 8 * half + 8)
            for s, pieces in enumerate((even, odd) if half == 0 else (odd, even)):
                taken = next(t for t in (matched(c, pieces, ranks, m) for m in range(12)) if t)
                for k, p in taken.items():
                    routes[s].append((c * 16 + p, k * 16 + c))
                    slots[half, c, p] = 16 + 8 * (k % 2) + 2 * (k // 2 % 4) + s
    return routes, slots


def transposed(x):
    pairs = [(a * 16 + b, b * 16 + a) for a in range(16) for b in range(16)]
    return lax.ppermute(x, ("row", "col"), pairs)


def across(x):
    return lax.ppermute(x, "row", [(a, (a + 8) % 16) for a in range(16)])


def along_x(x, shift):
    return lax.ppermute(x, "col", [(a, (a + 4 * shift) % 16) for a in range(16)])


def along_y(x, shift):
    return lax.ppermute(x, "row", [(a, a // 8 * 8 + (a + 2 * shift) % 8) for a in range(16)])


def along_z(x, flip):
    return lax.ppermute(x, "col", [(a, a ^ flip) for a in range(16)])


def swapped(x):
    return lax.ppermute(x, "row", [(a, a ^ 1) for a in range(16)])


def gathered(own, both):
    line = jnp.stack([own, *(along_z(own, f) for f in (1, 2, 3))])
    line, both = lax.optimization_barrier((line, both))
    groups = [along_x(line, s) for s in SHIFTS]
    cols = (both, *(along_y(both, s) for s in SHIFTS))
    twin = jnp.stack(cols)
    *groups, twin = lax.optimization_barrier((*groups, twin))
    return line, *groups, *cols, swapped(twin)


def reduced(*parts):
    rows, cols, twin = parts[:4], parts[4:8], swapped(parts[8])
    line = rows[0]
    for part, s in zip(rows[1:], SHIFTS):
        line = line + along_x(part, s)
    mine = [c + t for c, t in zip(cols, twin)]
    total = mine[0]
    for part, s in zip(mine[1:], SHIFTS):
        total = total + along_y(part, s)
    row_sum = line[0]
    for f in (1, 2, 3):
        row_sum = row_sum + along_z(line[f], f)
    return row_sum, total


def local(coords, dissimilarity):
    row, col = lax.axis_index("row"), lax.axis_index("col")
    lead_base = jnp.where(row > col, BLOCK, 0)
    trail_base = jnp.where(row < col, BLOCK, jnp.where(row > col, HALF, 0))
    diagonal = (row == col).astype(jnp.int32)
    line, half = col % 4, row // 8
    routes, slots = short_routes()
    piece = jnp.arange(16, dtype=jnp.int32)
    row_slots = piece // 4 * 4 + jnp.bitwise_xor(piece % 4, line)
    even_slots = 16 + 8 * (piece % 2) + piece // 2 % 4 * 2 + jnp.bitwise_xor(piece // 8, half)
    short_slots = jnp.asarray(slots)[half, col]
    head = jnp.stack([lead_base, trail_base, diagonal, col // 4, row // 2 % 4, row % 2]).astype(jnp.int32)
    scale = 1.0 / SAMPLES
    own = coords
    both = jnp.stack([lax.ppermute(coords, ("row", "col"), r) for r in routes])
    for iteration in range(ITERS):
        came_slots = even_slots if iteration else short_slots
        gone_slots = even_slots if iteration + 1 < ITERS else short_slots
        where = jnp.concatenate([head, row_slots, came_slots, row_slots, gone_slots]).astype(jnp.int32)
        parts = tile_terms(where, dissimilarity, *gathered(own, both))
        row_sum, total = reduced(*parts)
        if iteration + 1 < ITERS:
            col_sum = total[0] + across(total[1])
            came = transposed(jnp.stack([row_sum, col_sum]))
            own = (row_sum + came[1]) * scale
            turned = (col_sum + came[0]) * scale
            both = jnp.stack([turned, across(turned)])
        else:
            for part, route in zip(total, routes):
                row_sum = row_sum + lax.ppermute(part, ("row", "col"), [(b, a) for a, b in route])
            own = row_sum * scale
    return own


def solution(mesh):
    in_specs = (P(None, ("row", "col")), P("row", "col"))
    out_specs = P(None, ("row", "col"))
    return jax.shard_map(local, mesh=mesh, in_specs=in_specs, out_specs=out_specs, check_vma=False)
```

```python
import jax
import jax.numpy as jnp
import numpy as np
from jax import lax
from jax.experimental import pallas as pl
from jax.experimental.pallas import tpu as pltpu
from jax.sharding import PartitionSpec as P

ITERS = 2
DIMS = 64
PIECE = 128
CHUNK = 256
TALL = 512
WIDE = 512
HALF = 4
STEPS = 4
BLOCK = 8
STACK = 3 * DIMS + 16
HEAD = 6
SAMPLES = 32768

SHIFTS = (1, 3, 2)


def nn(a, b):
    return lax.dot_general(a, b, (((1,), (0,)), ((), ())), preferred_element_type=jnp.float32)


def tile_kernel(where_ref, values_hbm, *refs):
    sources, targets = refs[:9], refs[9:18]
    given, made, values_ref, left, right, stack, table, norm_i, norm_j, acc, acc_lead = refs[18:29]
    value_sem, coord_sem, term_sem = refs[29:]
    lead_base, trail_base, diagonal = where_ref[0], where_ref[1], where_ref[2]
    x_pos, y_pos, core = where_ref[3], where_ref[4], where_ref[5]

    def at(n, length=CHUNK):
        return pl.ds(pl.multiple_of(n * CHUNK, CHUNK), length)

    def band(step):
        return pl.ds(pl.multiple_of(step * TALL, TALL), TALL)

    def value_copy(step):
        return pltpu.make_async_copy(values_hbm.at[band(step)], values_ref.at[band(step)], value_sem.at[step])

    def moves(refs, send):
        for t, shift in enumerate((0, *SHIFTS)):
            group = lax.rem(x_pos + (shift if send else 4 - shift), 4)
            yield pl.ds(4 * group, 4), refs[t]
        for t, shift in enumerate((0, *SHIFTS)):
            y = lax.rem(y_pos + (shift if send else 4 - shift), 4)
            yield pl.ds(16 + 8 * core + 2 * y, 2), refs[4 + t]
            yield pl.ds(16 + 8 * (1 - core) + 2 * y, 2), refs[8].at[t]

    coord_copies = [
        pltpu.make_async_copy(ref, given.at[slots], coord_sem.at[k]) for k, (slots, ref) in enumerate(moves(sources, False))
    ]
    term_copies = [
        pltpu.make_async_copy(made.at[slots], ref, term_sem.at[k]) for k, (slots, ref) in enumerate(moves(targets, True))
    ]

    for copy in coord_copies:
        copy.start()
    for step in range(STEPS):
        value_copy(step).start()
    acc[...] = jnp.zeros_like(acc)
    acc_lead[...] = jnp.zeros_like(acc_lead)
    for copy in coord_copies:
        copy.wait()

    def coords_of(n):
        return jnp.concatenate([given[where_ref[HEAD + 2 * n]], given[where_ref[HEAD + 2 * n + 1]]], axis=1)

    def split(n):
        x = coords_of(n)
        hi = x.astype(jnp.bfloat16)
        hi32 = hi.astype(jnp.float32)
        rest = x - hi32
        mid = rest.astype(jnp.bfloat16)
        mid32 = mid.astype(jnp.float32)
        lo = (rest - mid32).astype(jnp.bfloat16)
        near = hi32 + mid32
        norms = jnp.sum(near * near, axis=0, keepdims=True)
        main = jnp.concatenate([hi32, mid32], axis=0).T.astype(jnp.bfloat16)
        return hi, mid, lo, norms, main

    for k in range(BLOCK):
        n = lead_base + k
        hi, mid, lo, norms, main = split(n)
        stack[:, at(k)] = jnp.concatenate([hi, mid, lo, jnp.ones((16, CHUNK), jnp.bfloat16)], axis=0)
        left[at(k), :] = jnp.concatenate([main, main], axis=1)
        norm_i[at(k), :] = jnp.broadcast_to(norms, (PIECE, CHUNK)).T

    def trail_chunk(n):
        hi, mid, lo, norms, main = split(n)
        right[:, at(n)] = -2.0 * jnp.concatenate([hi, mid, mid, hi], axis=0)
        lo32 = lo.astype(jnp.float32)
        tail = jnp.concatenate([lo32, jnp.ones_like(lo32)], axis=0).T.astype(jnp.bfloat16)
        table[at(n), :] = jnp.concatenate([main, tail], axis=1)
        norm_j[:, at(n)] = jnp.broadcast_to(norms + 1.0, (8, CHUNK))

    for k in range(HALF):
        trail_chunk(trail_base + k)

    @pl.when(diagonal == 1)
    def _():
        @pl.loop(HALF, BLOCK)
        def _(k):
            trail_chunk(k)

    def ratios_of(values, lead, trail):
        inner = nn(left[at(lead - lead_base, TALL), :], right[:, at(trail, WIDE)])
        ni = jnp.concatenate([norm_i[at(lead - lead_base, TALL), :]] * (WIDE // PIECE), axis=1)
        squared = inner + (ni + norm_j[0:1, at(trail, WIDE)])
        return values * lax.rsqrt(squared)

    def products(ratios, lead, trail):
        hi = ratios.astype(jnp.bfloat16)
        lo = (ratios - hi.astype(jnp.float32)).astype(jnp.bfloat16)
        above, beside = stack[:, at(lead - lead_base, TALL)], table[at(trail, WIDE), :]
        acc[:, at(trail, WIDE)] += nn(above, hi) + nn(above, lo)
        acc_lead[at(lead - lead_base, TALL), :] += nn(hi, beside) + nn(lo, beside)

    def values_at(step, j):
        return values_ref[band(step), j * WIDE : (j + 1) * WIDE]

    @pl.loop(0, STEPS // 2)
    def _(pair):
        value_copy(2 * pair).wait()
        value_copy(2 * pair + 1).wait()
        special = jnp.logical_and(diagonal == 1, pair == 0)

        @pl.when(jnp.logical_not(special))
        def _():
            for i in range(2):
                step = 2 * pair + i
                lead = lead_base + 2 * step
                for j in range(2):
                    trail = trail_base + 2 * j
                    products(ratios_of(values_at(step, j), lead, trail), lead, trail)

        @pl.when(special)
        def _():
            ahead = lax.broadcasted_iota(jnp.int32, (TALL, WIDE), 1) - lax.broadcasted_iota(jnp.int32, (TALL, WIDE), 0)
            for step, j, late in ((0, 0, 0), (0, 1, 0), (0, 0, 1), (1, 1, 0), (1, 0, 1), (1, 1, 1)):
                lead, trail = 2 * step + HALF * late, 2 * j + HALF * late
                ratios = ratios_of(values_at(step, j), lead, trail)
                if step == j:
                    ratios = jnp.where(ahead < 0 if late else ahead > 0, ratios, 0.0)
                products(ratios, lead, trail)

    low_lanes = lax.broadcasted_iota(jnp.int32, (CHUNK, PIECE), 1) < DIMS
    for n in range(BLOCK):
        near, far = acc_lead[n * CHUNK : (n + 1) * CHUNK, :PIECE], acc_lead[n * CHUNK : (n + 1) * CHUNK, PIECE:]
        folded = jnp.where(low_lanes, near + pltpu.roll(near, DIMS, 1) + far, far).T
        acc[:DIMS, at(lead_base + n)] += folded[:DIMS]
        acc[3 * DIMS :, at(lead_base + n)] += folded[DIMS : DIMS + 16]
    for n in range(2 * BLOCK):
        part = acc[:, at(n)]
        pulled = part[0:DIMS] + part[DIMS : 2 * DIMS] + part[2 * DIMS : 3 * DIMS]
        terms = coords_of(n) * part[3 * DIMS : 3 * DIMS + 1] - pulled
        made[where_ref[HEAD + 32 + 2 * n]] = terms[:, :PIECE]
        made[where_ref[HEAD + 33 + 2 * n]] = terms[:, PIECE:]
        if n == BLOCK - 1:
            for copy in term_copies[:4]:
                copy.start()
    for copy in term_copies[4:]:
        copy.start()
    for copy in term_copies:
        copy.wait()


def tile_terms(where, values, *coords):
    shapes = tuple(jax.ShapeDtypeStruct(x.shape, jnp.float32) for x in coords)
    total = 2 * BLOCK * CHUNK
    anywhere = pl.BlockSpec(memory_space=pl.ANY)
    pieces = pltpu.VMEM((32, DIMS, PIECE), jnp.float32)
    return pl.pallas_call(
        tile_kernel,
        out_shape=shapes,
        in_specs=[pl.BlockSpec(memory_space=pltpu.SMEM)] + [anywhere] * (1 + len(coords)),
        out_specs=(anywhere,) * len(coords),
        scratch_shapes=[
            pieces,
            pieces,
            pltpu.VMEM(values.shape, jnp.float32),
            pltpu.VMEM((total // 2, CHUNK), jnp.bfloat16),
            pltpu.VMEM((CHUNK, total), jnp.bfloat16),
            pltpu.VMEM((STACK, total // 2), jnp.bfloat16),
            pltpu.VMEM((total, CHUNK), jnp.bfloat16),
            pltpu.VMEM((total // 2, PIECE), jnp.float32),
            pltpu.VMEM((8, total), jnp.float32),
            pltpu.VMEM((STACK, total), jnp.float32),
            pltpu.VMEM((total // 2, CHUNK), jnp.float32),
            pltpu.SemaphoreType.DMA((STEPS,)),
            pltpu.SemaphoreType.DMA((12,)),
            pltpu.SemaphoreType.DMA((12,)),
        ],
        compiler_params=pltpu.CompilerParams(vmem_limit_bytes=48 * 1024 * 1024),
        cost_estimate=pl.CostEstimate(flops=6_000_000_000, transcendentals=2_097_152, bytes_accessed=10_000_000),
    )(where, values, *coords)


def short_routes():
    def hops(c, p, k):
        def ring(a, b, n):
            return min((a - b) % n, (b - a) % n)

        across_x, across_y = ring(p // 4, c // 4, 4), ring(c // 2 % 4, k // 2 % 4, 4)
        return across_x + across_y + ring(c // 8 * 4 + p % 4, k // 8 * 4 + c % 4, 8)

    def matched(c, pieces, ranks, most):
        taken = {}

        def place(p, seen):
            for k in ranks:
                if k not in seen and hops(c, p, k) <= most:
                    seen.add(k)
                    if k not in taken or place(taken[k], seen):
                        taken[k] = p
                        return True
            return False

        return taken if all(place(p, set()) for p in pieces) else None

    routes, slots = ([], []), np.zeros((2, 16, 16), np.int32)
    for c in range(16):
        even = [p for p in range(16) if (p // 4 + p % 4) % 2 == 0]
        odd = [p for p in range(16) if p not in even]
        for half in range(2):
            ranks = range(8 * half, 8 * half + 8)
            for s, pieces in enumerate((even, odd) if half == 0 else (odd, even)):
                taken = next(t for t in (matched(c, pieces, ranks, m) for m in range(12)) if t)
                for k, p in taken.items():
                    routes[s].append((c * 16 + p, k * 16 + c))
                    slots[half, c, p] = 16 + 8 * (k % 2) + 2 * (k // 2 % 4) + s
    return routes, slots


def transposed(x):
    pairs = [(a * 16 + b, b * 16 + a) for a in range(16) for b in range(16)]
    return lax.ppermute(x, ("row", "col"), pairs)


def across(x):
    return lax.ppermute(x, "row", [(a, (a + 8) % 16) for a in range(16)])


def along_x(x, shift):
    return lax.ppermute(x, "col", [(a, (a + 4 * shift) % 16) for a in range(16)])


def along_y(x, shift):
    return lax.ppermute(x, "row", [(a, a // 8 * 8 + (a + 2 * shift) % 8) for a in range(16)])


def along_z(x, flip):
    return lax.ppermute(x, "col", [(a, a ^ flip) for a in range(16)])


def swapped(x):
    return lax.ppermute(x, "row", [(a, a ^ 1) for a in range(16)])


def gathered(own, both):
    line = jnp.stack([own, *(along_z(own, f) for f in (1, 2, 3))])
    groups = [along_x(line, s) for s in SHIFTS]
    cols = (both, *(along_y(both, s) for s in SHIFTS))
    twin = jnp.stack(cols)
    *groups, twin = lax.optimization_barrier((*groups, twin))
    return line, *groups, *cols, swapped(twin)


def reduced(*parts):
    rows, cols, twin = parts[:4], parts[4:8], swapped(parts[8])
    line = rows[0]
    for part, s in zip(rows[1:], SHIFTS):
        line = line + along_x(part, s)
    mine = [c + t for c, t in zip(cols, twin)]
    total = mine[0]
    for part, s in zip(mine[1:], SHIFTS):
        total = total + along_y(part, s)
    line, total = lax.optimization_barrier((line, total))
    row_sum = line[0]
    for f in (1, 2, 3):
        row_sum = row_sum + along_z(line[f], f)
    return row_sum, total


def local(coords, dissimilarity):
    row, col = lax.axis_index("row"), lax.axis_index("col")
    lead_base = jnp.where(row > col, BLOCK, 0)
    trail_base = jnp.where(row < col, BLOCK, jnp.where(row > col, HALF, 0))
    diagonal = (row == col).astype(jnp.int32)
    line, half = col % 4, row // 8
    routes, slots = short_routes()
    piece = jnp.arange(16, dtype=jnp.int32)
    row_slots = piece // 4 * 4 + jnp.bitwise_xor(piece % 4, line)
    even_slots = 16 + 8 * (piece % 2) + piece // 2 % 4 * 2 + jnp.bitwise_xor(piece // 8, half)
    short_slots = jnp.asarray(slots)[half, col]
    head = jnp.stack([lead_base, trail_base, diagonal, col // 4, row // 2 % 4, row % 2]).astype(jnp.int32)
    scale = 1.0 / SAMPLES
    own = coords
    both = jnp.stack([lax.ppermute(coords, ("row", "col"), r) for r in routes])
    for iteration in range(ITERS):
        came_slots = even_slots if iteration else short_slots
        gone_slots = even_slots if iteration + 1 < ITERS else short_slots
        where = jnp.concatenate([head, row_slots, came_slots, row_slots, gone_slots]).astype(jnp.int32)
        parts = tile_terms(where, dissimilarity, *gathered(own, both))
        row_sum, total = reduced(*parts)
        if iteration + 1 < ITERS:
            col_sum = total[0] + across(total[1])
            came = transposed(jnp.stack([row_sum, col_sum]))
            own = (row_sum + came[1]) * scale
            turned = (col_sum + came[0]) * scale
            both = jnp.stack([turned, across(turned)])
        else:
            for part, route in zip(total, routes):
                row_sum = row_sum + lax.ppermute(part, ("row", "col"), [(b, a) for a, b in route])
            own = row_sum * scale
    return own


def solution(mesh):
    in_specs = (P(None, ("row", "col")), P("row", "col"))
    out_specs = P(None, ("row", "col"))
    return jax.shard_map(local, mesh=mesh, in_specs=in_specs, out_specs=out_specs, check_vma=False)
```
